128 devices in a mesh: dp: 8 (over y_hi, x), row: 4 (over z), col: 4 (over y_lo, core).
Axes of the slice: x: 4, y: 4 (y_hi: 2, y_lo: 2; y = y_hi * 2 + y_lo), z: 4, core: 2. Of those that a mesh axis runs over, the one named last changes fastest.
Arguments:
- tokens: bfloat16 [8192, 2048], P(('dp', 'col'), 'row'), may hold values from -6 to 6
- documents: int32 [8, 1024], P('dp'), may hold values from 0 to 3, never falling along the last dimension, each value on 1 to 512 neighbouring positions
- piece_starts: int32 [8, 2], P('dp'), may hold values from 0 to 768, as said below
- latent_down: bfloat16 [2048, 1024], P('row'), may hold values from -0.125 to 0.125
- key_value: bfloat16 [2048, 512], P('row'), may hold values from -0.125 to 0.125
- query_up: bfloat16 [1024, 4096], P(None, 'row'), may hold values from -0.1875 to 0.1875
- output_weight: bfloat16 [4096, 2048], P('row', 'col'), may hold values from -0.75 to 0.75
- gate_weight: bfloat16 [2048, 5632], P('row', 'col'), may hold values from -0.125 to 0.125
- up_weight: bfloat16 [2048, 5632], P('row', 'col'), may hold values from -0.125 to 0.125
- down_weight: bfloat16 [5632, 2048], P('col', 'row'), may hold values from -0.15625 to 0.15625
- input_gain: float32 [2048], P('row'), may hold values from 0.5 to 1.5
- latent_gain: float32 [1024], replicated, may hold values from 0.5 to 1.5
- middle_gain: float32 [2048], P('row'), may hold values from 0.5 to 1.5
- cotangent: bfloat16 [8192, 2048], P(('dp', 'col'), 'row'), may hold values from -6 to 6
Outputs:
- layer_out: bfloat16 [8192, 2048], P(('dp', 'col'), 'row')
- grad_tokens: bfloat16 [8192, 2048], P(('dp', 'col'), 'row')
- grad_latent_down: float32 [2048, 1024], P('row')
- grad_key_value: float32 [2048, 512], P('row')
- grad_query_up: float32 [1024, 4096], P(None, 'row')
- grad_output_weight: float32 [4096, 2048], P('row', 'col')
- grad_gate_weight: float32 [2048, 5632], P('row', 'col')
- grad_up_weight: float32 [2048, 5632], P('row', 'col')
- grad_down_weight: float32 [5632, 2048], P('col', 'row')
- grad_input_gain: float32 [2048], P('row')
- grad_latent_gain: float32 [1024], replicated
- grad_middle_gain: float32 [2048], P('row')
The draws below stay inside these ranges and needn't reach their ends.
Inputs may be any that keep to these rules, and one draw needn't show every extreme that they name: `documents`: within each sequence the document numbers never fall; each document has 1 to 512 tokens. `piece_starts`: piece m of a sequence starts in the m-th of 2 equal zones of the sequence and ends inside that zone; the first sequence has a piece at its start and one at its end.
All inputs are finite; a program needn't handle non-finite values.
Results may differ from the reference program's by a relative error of at most 0.033.
Values may be sent and summed in bfloat16 or wider, within the bound.
A program may use at most 128 MiB of HBM per device.

```python
import math
import jax
import jax.numpy as jnp
import numpy as np
from jax import lax

D = 2048
HEADS = 16
HDIM = 256
LAT = 1024
FF = 5632
SEQ = 1024
PIECE = 256
PIECES = 2
DOCS = 4
ROWS = 8
TOKENS = 8192


def draw_piece_starts(key, part):
    zone_width = SEQ // PIECES
    offsets = jax.random.randint(key, (ROWS, PIECES), 0, zone_width - PIECE + 1, dtype=jnp.int32)
    starts = offsets + (jnp.arange(PIECES, dtype=jnp.int32) * zone_width)[None, :]
    starts = starts.at[0, 0].set(0)
    starts = starts.at[0, PIECES - 1].set(SEQ - PIECE)
    return starts


def level_of(rng, dims, split, low, largest):
    gain, own = 1.0, jax.random.fold_in(rng, 6)
    for dim, blocks in split:
        steps = jnp.exp(jax.random.uniform(jax.random.fold_in(own, dim), (blocks,), jnp.float32, low / len(split), largest / len(split)))
        gain = gain * jnp.repeat(steps, dims[dim] // blocks).reshape([-1 if axis == dim else 1 for axis in range(len(dims))])
    return gain


def split_up(amount, total, bound, skew):
    portions = [(1 << 20) // math.isqrt(standing ** skew) + 1 for standing in range(2, amount + 1)]
    surplus, holding = total - bound - (amount - 1), [1] * (amount - 1)
    while surplus > 0:
        free = [i for i in range(amount - 1) if holding[i] < bound]
        whole, remaining = sum([portions[i] for i in free]), surplus
        for i in free:
            extra = min(bound - holding[i], max(1, remaining * portions[i] // whole), surplus)
            holding[i] = holding[i] + extra
            surplus = surplus - extra
    return np.array([bound] + holding)


def uneven_parts(key, amount, total, bound, slope):
    if amount == 2:
        one = jax.random.randint(key, (), max(1, total - bound), min(bound, total - 1) + 1)
        return jnp.stack([one, total - one])
    tallies = jnp.asarray(split_up(amount, total, bound, slope), jnp.int32)
    twos = (amount - 1) // 2
    donor, taker = tallies[1:1 + 2 * twos:2], tallies[2:2 + 2 * twos:2]
    margin = jnp.minimum(donor - 1, bound - taker)
    moved = jax.random.randint(jax.random.fold_in(key, 1), (twos,), 0, 1 << 20) % (margin + 1)
    tallies = tallies.at[1:1 + 2 * twos:2].set(donor - moved).at[2:2 + 2 * twos:2].set(taker + moved)
    return tallies[jax.random.permutation(jax.random.fold_in(key, 2), amount)]


def centred(key, dims, deviation, reach, shards=(), kind=jnp.bfloat16):
    factor_of = level_of(key, dims, shards, -0.22, 0.18) if shards else 1.0
    entries = jax.random.normal(key, dims, jnp.float32) * deviation * factor_of
    return jnp.minimum(jnp.maximum(entries, -reach), reach).astype(kind)


def setup_inputs(seed: int = 0) -> dict:
    streams_of = jax.random.split(jax.random.key(seed), 15)
    return {
        "tokens": centred(streams_of[0], (TOKENS, D), 1.0, 6.0, ((0, 32), (1, 4))),
        "documents": jax.vmap(lambda own: jnp.searchsorted(jnp.cumsum(uneven_parts(own, DOCS, SEQ, SEQ // 2, 1)), jnp.arange(SEQ), side="right"))(jax.random.split(streams_of[1], ROWS)).reshape((ROWS, SEQ)).astype(jnp.int32),
        "piece_starts": draw_piece_starts(jax.random.fold_in(streams_of[14], 71), 0),
        "latent_down": centred(streams_of[3], (D, LAT), D ** -0.5, 0.125, ((0, 4),)),
        "key_value": centred(streams_of[4], (D, 2 * HDIM), D ** -0.5, 0.125, ((0, 4),)),
        "query_up": centred(streams_of[5], (LAT, HEADS * HDIM), LAT ** -0.5, 0.1875, ((1, 4),)),
        "output_weight": centred(streams_of[6], (HEADS * HDIM, D), (HEADS * HDIM // 64) ** -0.5, 0.75, ((0, 4), (1, 4))),
        "gate_weight": centred(streams_of[7], (D, FF), D ** -0.5, 0.125, ((0, 4), (1, 4))),
        "up_weight": centred(streams_of[8], (D, FF), D ** -0.5, 0.125, ((0, 4), (1, 4))),
        "down_weight": centred(streams_of[9], (FF, D), (FF // 4) ** -0.5, 0.15625, ((0, 4), (1, 4))),
        "input_gain": jnp.clip(1.0 + 0.1 * jax.random.normal(streams_of[10], (D,), jnp.float32), 0.5, 1.5),
        "latent_gain": jnp.clip(1.0 + 0.1 * jax.random.normal(streams_of[11], (LAT,), jnp.float32), 0.5, 1.5),
        "middle_gain": jnp.clip(1.0 + 0.1 * jax.random.normal(streams_of[12], (D,), jnp.float32), 0.5, 1.5),
        "cotangent": centred(streams_of[13], (TOKENS, D), 1.0, 6.0, ((0, 32), (1, 4))),
    }


epsilon = 1e-06
masked_value = -1e+30

@jax.custom_vjp
def low(v):
    return lax.optimization_barrier(v.astype(jnp.bfloat16)).astype(jnp.float32)

@jax.custom_vjp
def low_back(v):
    return v

def low_keep(v):
    return (low(v), None)

def low_pass(kept, grad):
    return (grad,)

def back_keep(v):
    return (v, None)

def back_low(kept, grad):
    return (low(grad),)
low.defvjp(low_keep, low_pass)
low_back.defvjp(back_keep, back_low)

def product(left, right):
    return jnp.dot(left, right, precision=lax.Precision.HIGHEST, preferred_element_type=jnp.float32)

def rope_tables(positions, width):
    half_width = width // 2
    frequency = jnp.exp(-math.log(10000.0) * jnp.arange(half_width, dtype=jnp.float32) / half_width)
    angles = positions.astype(jnp.float32)[:, None] * frequency[None, :]
    cosine = jnp.cos(angles)
    sine_part = jnp.sin(angles)
    return (jnp.concatenate([cosine, cosine], axis=1), jnp.concatenate([sine_part, sine_part], axis=1))

def rotate(values, cosine, sine_part):
    half_width = values.shape[-1] // 2
    turned = jnp.concatenate([-values[..., half_width:], values[..., :half_width]], axis=-1)
    return values * cosine + turned * sine_part

def piece_labels(positions, starts_row):
    inside = (positions[:, None] >= starts_row[None, :]) & (positions[:, None] < starts_row[None, :] + PIECE)
    numbers = jnp.arange(1, starts_row.shape[0] + 1, dtype=jnp.int32)
    return lax.optimization_barrier(jnp.sum(jnp.where(inside, numbers[None, :], 0), axis=1)) - 1

def allowed(query_place, key_place, query_doc, key_doc, starts_row):
    query_piece = piece_labels(query_place, starts_row)
    key_piece = piece_labels(key_place, starts_row)
    same_doc = query_doc[:, None] == key_doc[None, :]
    causal = key_place[None, :] <= query_place[:, None]
    same_piece = (query_piece[:, None] == key_piece[None, :]) & (query_piece[:, None] >= 0)
    return same_doc & (causal | same_piece)

def rms_scale(values):
    return lax.rsqrt(lax.optimization_barrier(jnp.mean(values * values, axis=-1, keepdims=True)) + epsilon)

def row_layer(params, row_in, doc_row, starts_row):
    latent_down, key_value, query_up, output_weight, gate_weight, up_weight, down_weight, input_gain, latent_gain, middle_gain = params
    normed = low(row_in * rms_scale(row_in) * input_gain)
    latent_all = low_back(jnp.concatenate([product(normed, latent_down), product(normed, key_value)], axis=1))
    latent = latent_all[:, :LAT]
    keys_raw = latent_all[:, LAT:LAT + HDIM]
    values_raw = latent_all[:, LAT + HDIM:]
    latent_normed = low(latent * rms_scale(latent) * latent_gain)
    query_raw = low_back(product(latent_normed, query_up)).reshape(SEQ, HEADS, HDIM)
    positions = jnp.arange(SEQ, dtype=jnp.int32)
    cosine, sine_part = rope_tables(positions, HDIM)
    queries = low(rotate(query_raw, cosine[:, None, :], sine_part[:, None, :]))
    keys = low(rotate(keys_raw, cosine, sine_part))
    values = low(values_raw)
    raw_scores = jnp.einsum('qhd,kd->qhk', queries, keys, precision=lax.Precision.HIGHEST)
    scores = low_back(raw_scores * (1.0 / math.sqrt(HDIM)))
    allowed_pairs = allowed(positions, positions, doc_row, doc_row, starts_row)
    masked = jnp.where(allowed_pairs[:, None, :], scores, masked_value)
    top_score = lax.optimization_barrier(jnp.max(masked, axis=2, keepdims=True))
    weights_raw = jnp.exp(masked - top_score)
    weights = weights_raw / lax.optimization_barrier(jnp.sum(weights_raw, axis=2, keepdims=True))
    mixed_heads = jnp.einsum('qhk,kd->qhd', low(weights), values, precision=lax.Precision.HIGHEST)
    mixed_low = low(low_back(mixed_heads.reshape(SEQ, HEADS * HDIM)))
    branch = low_back(product(mixed_low, output_weight))
    middle = row_in + branch
    normed_mid = low(middle * rms_scale(middle) * middle_gain)
    gate_val = low_back(product(normed_mid, gate_weight))
    up_val = low_back(product(normed_mid, up_weight))
    activated = low(jax.nn.silu(gate_val) * up_val)
    return middle + product(activated, down_weight)

def reference(tokens, documents, piece_starts, latent_down, key_value, query_up, output_weight, gate_weight, up_weight, down_weight, input_gain, latent_gain, middle_gain, cotangent):
    params = (latent_down.astype(jnp.float32), key_value.astype(jnp.float32), query_up.astype(jnp.float32), output_weight.astype(jnp.float32), gate_weight.astype(jnp.float32), up_weight.astype(jnp.float32), down_weight.astype(jnp.float32), input_gain.astype(jnp.float32), latent_gain.astype(jnp.float32), middle_gain.astype(jnp.float32))
    rows_in = tokens.astype(jnp.float32).reshape(ROWS, SEQ, D)
    checked_layer = jax.checkpoint(row_layer)

    def forward(weights_in, layer_in):

        def one_row(packed):
            return checked_layer(weights_in, packed[0], packed[1], packed[2])
        return lax.map(one_row, (layer_in, documents, piece_starts))
    result, pullback = jax.vjp(forward, params, rows_in)
    weight_grads, grad_rows = pullback(cotangent.astype(jnp.float32).reshape(ROWS, SEQ, D))
    return (result.reshape(TOKENS, D).astype(jnp.bfloat16), grad_rows.reshape(TOKENS, D).astype(jnp.bfloat16), weight_grads[0], weight_grads[1], weight_grads[2], weight_grads[3], weight_grads[4], weight_grads[5], weight_grads[6], weight_grads[7], weight_grads[8], weight_grads[9])
```

```python
import math

import jax
import jax.numpy as jnp
from jax import lax
from jax.experimental import pallas as pl
from jax.experimental.pallas import tpu as pltpu
from jax.sharding import PartitionSpec as P

D = 2048
SEQ = 1024
PIECE = 256
epsilon = 1e-06
masked_value = -1e30
F32 = jnp.float32
BF = jnp.bfloat16
MESH = pl.DeviceIdType.MESH
VM = pl.BlockSpec(memory_space=pltpu.VMEM)
SM = pl.BlockSpec(memory_space=pltpu.SMEM)
ANY = pl.BlockSpec(memory_space=pl.ANY)
NN = (((1,), (0,)), ((), ()))
NT = (((1,), (1,)), ((), ()))
TN = (((0,), (0,)), ((), ()))


def dot(a, b, dims=NN):
    return lax.dot_general(a, b, dims, preferred_element_type=F32)


class Links:
    def __init__(self, ssem, rsem, lsem):
        self.ssem, self.rsem, self.lsem = ssem, rsem, lsem
        self.n, self.m, self.open = 0, 0, []

    def send(self, src, dst, dev):
        c = pltpu.make_async_remote_copy(
            src_ref=src, dst_ref=dst, send_sem=self.ssem.at[self.n], recv_sem=self.rsem.at[self.n],
            device_id=dev, device_id_type=MESH)
        self.n += 1
        c.start()
        self.open.append(c)
        return c

    def local(self, src, dst):
        c = pltpu.make_async_copy(src, dst, self.lsem.at[self.m])
        self.m += 1
        c.start()
        return c

    def close(self):
        for c in self.open:
            c.wait_send()


def place():
    r, c = lax.axis_index("row"), lax.axis_index("col")
    core = {"col": c + 1 - 2 * lax.rem(c, 2)}
    yl = {"col": lax.rem(c + 2, 4)}
    zs = [{"row": lax.rem(r + k, 4)} for k in (1, 2, 3)]
    return r, c, core, yl, zs


def x_peers():
    p = lax.axis_index("dp")
    x = lax.rem(p, 4)
    return x, [{"dp": p - x + lax.rem(x + k, 4)} for k in (1, 2, 3)]


def blk(c):
    return pl.ds(pl.multiple_of(c * 256, 256), 256)


class Gather16:
    def __init__(self, net, buf):
        r, c, core, yl, zs = place()
        self.net, self.buf, self.at = net, buf, (r, c, core, yl, zs)

    def put(self, a, b, dev):
        v = self.buf.at[a, blk(b)]
        return self.net.send(v, v, dev)

    def first(self):
        r, c, core, yl, zs = self.at
        self.y = self.put(r, c, yl)
        self.z2 = self.put(r, c, zs[1])
        self.zp = self.put(r, c, zs[0])
        self.zm = self.put(r, c, zs[2])
        self.cores = [self.put(r, c, core)]

    def second(self):
        r, c, core, yl, zs = self.at
        far = lax.rem(c + 2, 4)
        self.y.wait_recv()
        self.yp = self.put(r, far, zs[0])
        self.ym = self.put(r, far, zs[2])
        self.cores.append(self.put(r, far, core))
        self.z2.wait_recv()
        self.zy = self.put(lax.rem(r + 2, 4), c, yl)
        self.cores.append(self.put(lax.rem(r + 2, 4), c, core))
        self.zp.wait_recv()
        self.cores.append(self.put(lax.rem(r + 3, 4), c, core))
        self.zm.wait_recv()
        self.cores.append(self.put(lax.rem(r + 1, 4), c, core))

    def third(self):
        r, c, core, yl, zs = self.at
        far = lax.rem(c + 2, 4)
        self.yp.wait_recv()
        self.cores.append(self.put(lax.rem(r + 3, 4), far, core))
        self.ym.wait_recv()
        self.cores.append(self.put(lax.rem(r + 1, 4), far, core))
        self.zy.wait_recv()
        self.cores.append(self.put(lax.rem(r + 2, 4), far, core))

    def last(self):
        for h in self.cores:
            h.wait_recv()


class Scatter16:
    def __init__(self, net, part, ctx, crx, tx, rx):
        self.net, self.part, self.at = net, part, place()
        self.ctx, self.crx, self.tx, self.rx = ctx, crx, tx, rx

    def first(self):
        r, c, core, yl, zs = self.at
        other = c + 1 - 2 * lax.rem(c, 2)
        self.cores = []
        for slot in (5, 7, 6, 1, 3, 2, 4, 0):
            b = other if slot < 4 else lax.rem(other + 2, 4)
            self.ctx[slot] = self.part(slot % 4, b).astype(BF)
            self.cores.append((slot, self.net.send(self.ctx.at[slot], self.crx.at[slot], core)))
        self.cores = dict(self.cores)

    def mine(self, slot):
        r, c, core, yl, zs = self.at
        b = c if slot < 4 else lax.rem(c + 2, 4)
        own = self.part(slot % 4, b)
        self.cores[slot].wait_recv()
        return own + self.crx[slot].astype(F32)

    def go(self, i, value, dev):
        self.tx[i] = value.astype(BF)
        return self.net.send(self.tx.at[i], self.rx.at[i], dev)

    def take(self, i, h):
        h.wait_recv()
        return self.rx[i].astype(F32)

    def second(self):
        r, c, core, yl, zs = self.at
        self.bp = self.go(0, self.mine(5), zs[0])
        self.bm = self.go(1, self.mine(7), zs[2])
        self.a = self.go(2, self.mine(6), yl)
        self.cp = self.go(3, self.mine(1), zs[0])
        self.cm = self.go(4, self.mine(3), zs[2])

    def third(self):
        r, c, core, yl, zs = self.at
        t = self.mine(2)
        self.d = self.go(5, t + self.take(2, self.a), zs[1])
        t = self.mine(4)
        self.e = self.go(6, t + self.take(0, self.bp) + self.take(1, self.bm), yl)

    def last(self):
        t = self.mine(0)
        for i, h in ((3, self.cp), (4, self.cm), (5, self.d), (6, self.e)):
            t = t + self.take(i, h)
        return t


class Weights:
    def __init__(self, net, gate, up, down, gu, dn):
        self.net, self.gate, self.up, self.down, self.gu, self.dn = net, gate, up, down, gu, dn
        self.x, self.xs = x_peers()

    def own(self):
        r = lax.axis_index("row")
        lanes = pl.ds(pl.multiple_of(r * 384, 128), 384)
        self.locals = [
            self.net.local(self.gate.at[:, lanes], self.gu.at[0, :, pl.ds(0, 384)]),
            self.net.local(self.up.at[:, lanes], self.gu.at[0, :, pl.ds(384, 384)]),
            self.net.local(self.down.at[pl.ds(pl.multiple_of(r * 384, 128), 384)], self.dn.at[0])]

    def first(self):
        r, c, core, yl, zs = place()
        x, net = self.x, self.net
        rows = pl.ds(pl.multiple_of(x * 128, 128), 128)
        self.z = []
        for k in (2, 1, 3):
            d = lax.rem(r + k, 4)
            lanes = pl.ds(pl.multiple_of(d * 384, 128), 384)
            drows = pl.ds(pl.multiple_of(d * 384 + x * 96, 32), 96)
            slot = 4 - k
            self.z += [
                net.send(self.gate.at[rows, lanes], self.gu.at[slot, rows, pl.ds(0, 384)], zs[k - 1]),
                net.send(self.up.at[rows, lanes], self.gu.at[slot, rows, pl.ds(384, 384)], zs[k - 1]),
                net.send(self.down.at[drows], self.dn.at[slot, pl.ds(pl.multiple_of(x * 96, 32), 96)], zs[k - 1])]

    def second(self):
        x, net = self.x, self.net
        for h in self.z:
            h.wait_recv()
        g = self.gu.at[pl.ds(1, 3), pl.ds(pl.multiple_of(x * 128, 128), 128)]
        d = self.dn.at[pl.ds(1, 3), pl.ds(pl.multiple_of(x * 96, 32), 96)]
        self.h = []
        for k in (2, 1, 3):
            self.h += [net.send(g, g, self.xs[k - 1]), net.send(d, d, self.xs[k - 1])]

    def last(self):
        for h in self.h:
            h.wait_recv()
        for h in self.locals:
            h.wait()


def meet(peers):
    b = pltpu.get_barrier_semaphore()
    for p in peers:
        pl.semaphore_signal(b, inc=1, device_id=p, device_id_type=MESH)
    pl.semaphore_wait(b, len(peers))


def pack_stat(s, lanes=128):
    hi = s.astype(BF).astype(F32)
    lo = (s - hi).astype(BF).astype(F32)
    rest = s - hi - lo
    lane = lax.broadcasted_iota(jnp.int32, (s.shape[0], lanes), 1)
    return jnp.where(lane == 0, hi, jnp.where(lane == 1, lo, jnp.where(lane == 2, rest, 0.0))).astype(BF)


def unpack_stat(t):
    return jnp.sum(t.astype(F32), axis=1, keepdims=True)


def rope(u, cos, sin):
    a, b = u[:, :128], u[:, 128:]
    return jnp.concatenate([a * cos - b * sin, b * cos + a * sin], axis=1)


def unrope(g, cos, sin):
    a, b = g[:, :128], g[:, 128:]
    return jnp.concatenate([a * cos + b * sin, b * cos - a * sin], axis=1)


def attn_fwd_kernel(x_ref, docs_ref, starts_ref, ld_ref, kvw_ref, qu_hbm, ow_hbm, ig_ref, lg_ref, mg_ref,
                    cos_ref, sin_ref, cot_ref, gate_hbm, up_hbm, down_hbm,
                    ln_ref, lat_ref, rlat_ref, q_ref, kv_ref, w_ref, mix_ref, oall_ref, mid_ref, nm_ref, rmid_ref,
                    gu_ref, dn_ref, call_ref,
                    pf, ps, prx, qu_v, bias, bp, brx, st_tx, st_rx, ssem, rsem, lsem):
    r, c, core, yl, zs = place()
    net = Links(ssem, rsem, lsem)
    meet(zs + [core, yl] + x_peers()[1])
    ow_own = net.local(ow_hbm, oall_ref.at[c])
    ow_yl = net.send(ow_hbm, oall_ref.at[c], yl)
    ow_core = net.send(ow_hbm, oall_ref.at[c], core)
    qu_in = net.local(qu_hbm, qu_v)
    ffw = Weights(net, gate_hbm, up_hbm, down_hbm, gu_ref, dn_ref)
    ffw.own()
    call_ref[r, blk(c)] = cot_ref[...]
    cots = Gather16(net, call_ref)

    x = x_ref[...].astype(F32)
    xg = (x * ig_ref[...]).astype(BF)
    ssq = jnp.sum(x * x, axis=1, keepdims=True)
    pf[:, :1024] = dot(xg, ld_ref[...])
    pf[:, 1024:1536] = dot(xg, kvw_ref[...])
    pf[:, 1536:] = jnp.broadcast_to(ssq, (256, 128))
    stat = pack_stat(ssq)
    for d in range(4):
        rows = slice(64 * d, 64 * d + 64)
        ps[d, :, :1536] = pf[rows, :1536].astype(BF)
        ps[d, :, 1536:] = stat[rows]
    got = []
    for k in (2, 1, 3):
        got.append(net.send(ps.at[lax.rem(r + k, 4)], prx.at[k - 1], zs[k - 1]))

    qpos = c * 256 + lax.broadcasted_iota(jnp.int32, (256, SEQ), 0)
    kpos = lax.broadcasted_iota(jnp.int32, (256, SEQ), 1)
    number = lax.broadcasted_iota(jnp.int32, (8, SEQ), 0)
    onehot = (jnp.broadcast_to(docs_ref[...], (8, SEQ)) == number).astype(F32)
    onehot_q = (jnp.broadcast_to(docs_ref[:, pl.ds(pl.multiple_of(c * 256, 256), 256)], (8, 256))
                == number[:, :256]).astype(F32)
    same_doc = dot(onehot_q, onehot, TN) > 0.5
    ok = kpos <= qpos
    for m in range(2):
        s = starts_ref[0, m]
        ok = ok | ((qpos >= s) & (qpos < s + PIECE) & (kpos >= s) & (kpos < s + PIECE))
    bias[...] = jnp.where(same_doc & ok, 0.0, masked_value)

    own = pl.ds(pl.multiple_of(r * 64, 64), 64)
    for g in got:
        g.wait_recv()
    total = pf[own, :1536]
    ss = pf[own, 1536:1537]
    for k in range(3):
        total = total + prx[k, :, :1536].astype(F32)
        ss = ss + unpack_stat(prx[k, :, 1536:])
    r_in = lax.rsqrt(ss / D + epsilon)
    total = total * r_in
    cos64, sin64 = cos_ref[own, :], sin_ref[own, :]
    kv_rows = pl.ds(pl.multiple_of(c * 256 + r * 64, 64), 64)
    kv_ref[kv_rows, :256] = rope(total[:, 1024:1280], cos64, sin64).astype(BF)
    kv_ref[kv_rows, 256:] = total[:, 1280:1536].astype(BF)
    kv_got = [net.send(kv_ref.at[kv_rows], kv_ref.at[kv_rows], zs[k - 1]) for k in (2, 1, 3)]
    lat = total[:, :1024]
    r_lat = lax.rsqrt(jnp.mean(lat * lat, axis=1, keepdims=True) + epsilon)
    ln_ref[r, :, :1024] = (lat * r_lat * lg_ref[...]).astype(BF)
    ln_ref[r, :, 1024:] = pack_stat(r_in)
    ln_got = [net.send(ln_ref.at[r], ln_ref.at[r], zs[k - 1]) for k in (2, 1, 3)]
    lat_ref[...] = lat
    rlat_ref[...] = jnp.broadcast_to(r_lat, (64, 128))
    for g in kv_got:
        g.wait_recv()
    own_kv = kv_ref.at[pl.ds(pl.multiple_of(c * 256, 256), 256)]
    kv_yl = net.send(own_kv, own_kv, yl)
    kv_core = net.send(own_kv, own_kv, core)
    for g in ln_got:
        g.wait_recv()
    ffw.first()
    cots.first()
    qu_in.wait()
    cos, sin = cos_ref[...], sin_ref[...]
    ln_all = ln_ref[:, :, :1024].reshape(256, 1024)

    def make_query(h, carry):
        u = dot(ln_all, qu_v[:, pl.ds(pl.multiple_of(h * 256, 256), 256)])
        q_ref[h] = (rope(u, cos, sin) * (1.0 / 16.0)).astype(BF)
        return carry

    lax.fori_loop(0, 4, make_query, 0)
    kv_yl.wait_recv()
    far_kv = kv_ref.at[pl.ds(pl.multiple_of(lax.rem(c + 2, 4) * 256, 256), 256)]
    kv_far = net.send(far_kv, far_kv, core)
    ow_yl.wait_recv()
    ow_far = net.send(oall_ref.at[lax.rem(c + 2, 4)], oall_ref.at[lax.rem(c + 2, 4)], core)
    kv_core.wait_recv()
    kv_far.wait_recv()

    def head(h, carry):
        s = dot(q_ref[h], kv_ref[:, :256], NT) + bias[...]
        top = jnp.max(s, axis=1, keepdims=True)
        e = jnp.exp(s - top)
        w = (e / jnp.sum(e, axis=1, keepdims=True)).astype(BF)
        w_ref[h] = w
        mix_ref[:, pl.ds(pl.multiple_of(h * 256, 256), 256)] = dot(w, kv_ref[:, 256:]).astype(BF)
        return carry

    lax.fori_loop(0, 4, head, 0)
    ffw.second()
    cots.second()
    ow_own.wait()
    ow_core.wait_recv()
    ow_far.wait_recv()
    got = []
    for k in (2, 1, 3):
        d = lax.rem(r + k, 4)
        bp[k - 1] = dot(mix_ref[...], oall_ref[d]).astype(BF)
        got.append(net.send(bp.at[k - 1], brx.at[k - 1], zs[k - 1]))
    branch = dot(mix_ref[...], oall_ref[r])
    for g in got:
        g.wait_recv()
    for k in range(3):
        branch = branch + brx[k].astype(F32)
    middle = x_ref[...].astype(F32) + branch
    mid_ref[...] = middle
    ssm = jnp.sum(middle * middle, axis=1, keepdims=True)
    st_tx[...] = jnp.broadcast_to(ssm, (256, 128))
    got = [net.send(st_tx, st_rx.at[k - 1], zs[k - 1]) for k in (2, 1, 3)]
    for g in got:
        g.wait_recv()
    for k in range(3):
        ssm = ssm + st_rx[k, :, :1]
    r_mid = lax.rsqrt(ssm / D + epsilon)
    rmid_ref[...] = jnp.broadcast_to(r_mid, (256, 128))
    nm_ref[...] = (middle * r_mid * mg_ref[...]).astype(BF)
    cots.third()
    cots.last()
    ffw.last()
    net.close()


def S(shape, dtype=BF):
    return jax.ShapeDtypeStruct(shape, dtype)


def attn_fwd(x, docs, starts, ld, kvw, qu, ow, ig, lg, mg, cos, sin, cot, gate, up, down):
    return pl.pallas_call(
        attn_fwd_kernel,
        out_shape=(S((4, 64, 1152)), S((64, 1024), F32), S((64, 128), F32), S((4, 256, 256)), S((1024, 512)),
                   S((4, 256, 1024)), S((256, 1024)), S((4, 1024, 512)), S((256, 512), F32), S((256, 512)),
                   S((256, 128), F32), S((4, 512, 768)), S((4, 384, 512)), S((4, 1024, 512))),
        in_specs=[VM, VM, SM, VM, VM, ANY, ANY, VM, VM, VM, VM, VM, VM, ANY, ANY, ANY],
        out_specs=(VM,) * 14,
        scratch_shapes=[
            pltpu.VMEM((256, 1664), F32), pltpu.VMEM((4, 64, 1664), BF), pltpu.VMEM((3, 64, 1664), BF),
            pltpu.VMEM((1024, 1024), BF), pltpu.VMEM((256, 1024), F32), pltpu.VMEM((3, 256, 512), BF),
            pltpu.VMEM((3, 256, 512), BF), pltpu.VMEM((256, 128), F32), pltpu.VMEM((3, 256, 128), F32),
            pltpu.SemaphoreType.DMA((64,)), pltpu.SemaphoreType.DMA((64,)), pltpu.SemaphoreType.DMA((8,))],
        compiler_params=pltpu.CompilerParams(collective_id=0, has_side_effects=True, vmem_limit_bytes=56 << 20),
        name="attn_fwd",
    )(x, docs, starts, ld, kvw, qu, ow, ig, lg, mg, cos, sin, cot, gate, up, down)


def own_rope(local_rows):
    places = lax.axis_index("col") * local_rows + jnp.arange(local_rows, dtype=jnp.int32)
    freq = jnp.exp(-math.log(10000.0) * jnp.arange(128, dtype=F32) / 128)
    ang = places.astype(F32)[:, None] * freq[None, :]
    return jnp.cos(ang), jnp.sin(ang)


def ffn_kernel(nm_ref, gu_ref, dn_ref, call_ref, mid_ref, rmid_ref, mg_ref,
               out_ref, gmid_ref, gain_ref, ggu_out, gdn_out,
               m_ref, act_ref, gg_ref, ctx1, crx1, tx1, rx1, ctx2, crx2, tx2, rx2, st_tx, st_rx, ssem, rsem, lsem):
    r, c, core, yl, zs = place()
    net = Links(ssem, rsem, lsem)
    m_ref[r, blk(c)] = nm_ref[...]
    meet(zs + [core, yl])
    gather = Gather16(net, m_ref)
    gather.first()
    gather.second()
    gather.third()
    gather.last()

    def tile(t, carry):
        rows = blk(t)
        gu = jnp.zeros((256, 768), F32)
        ga = jnp.zeros((256, 384), F32)
        for k in range(4):
            f = lax.rem(r + k, 4)
            gu = gu + dot(m_ref[f, rows], gu_ref[k])
            ga = ga + dot(call_ref[f, rows], dn_ref[k], NT)
        g, u = gu[:, :384], gu[:, 384:]
        sig = 1.0 / (1.0 + jnp.exp(-g))
        silu = g * sig
        act_ref[rows] = (silu * u).astype(BF)
        gg_ref[rows, :384] = (ga * u * sig * (1.0 + g * (1.0 - sig))).astype(BF)
        gg_ref[rows, 384:] = (ga * silu).astype(BF)
        return carry

    lax.fori_loop(0, 4, tile, 0)
    back = Scatter16(net, lambda k, b: dot(gg_ref[blk(b)], gu_ref[k], NT), ctx1, crx1, tx1, rx1)
    back.first()
    back.second()

    def grads(k, carry):
        f = lax.rem(r + k, 4)
        ggu_out[f] = dot(m_ref[f], gg_ref[...], TN).astype(BF)
        gdn_out[f] = dot(act_ref[...], call_ref[f], TN).astype(BF)
        return carry

    lax.fori_loop(0, 2, grads, 0)
    back.third()
    lax.fori_loop(2, 4, grads, 0)
    fwd = Scatter16(net, lambda k, b: dot(act_ref[blk(b)], dn_ref[k]), ctx2, crx2, tx2, rx2)
    fwd.first()
    gm = back.last()
    middle, r_mid = mid_ref[...], rmid_ref[:, :1]
    gained = gm * mg_ref[...]
    stat = jnp.sum(gained * middle, axis=1, keepdims=True)
    st_tx[...] = jnp.broadcast_to(stat, (256, 128))
    got = [net.send(st_tx, st_rx.at[k - 1], zs[k - 1]) for k in (2, 1, 3)]
    gain_ref[...] = jnp.sum(gm * middle * r_mid, axis=0, keepdims=True)
    fwd.second()
    for g in got:
        g.wait_recv()
    for k in range(3):
        stat = stat + st_rx[k, :, :1]
    gmid_ref[...] = call_ref[r, blk(c)].astype(F32) + r_mid * gained - middle * (r_mid * r_mid * r_mid * stat / D)
    fwd.third()
    out_ref[...] = (middle + fwd.last()).astype(BF)
    net.close()


def ffn(nm, gu, dn, call, mid, rmid, mg):
    big = [pltpu.VMEM((8, 256, 512), BF), pltpu.VMEM((8, 256, 512), BF), pltpu.VMEM((7, 256, 512), BF),
           pltpu.VMEM((7, 256, 512), BF)]
    return pl.pallas_call(
        ffn_kernel,
        out_shape=(S((256, 512)), S((256, 512), F32), S((1, 512), F32), S((4, 512, 768)), S((4, 384, 512))),
        in_specs=[VM] * 7,
        out_specs=(VM,) * 5,
        scratch_shapes=[pltpu.VMEM((4, 1024, 512), BF), pltpu.VMEM((1024, 384), BF), pltpu.VMEM((1024, 768), BF),
                        *big, *big, pltpu.VMEM((256, 128), F32), pltpu.VMEM((3, 256, 128), F32),
                        pltpu.SemaphoreType.DMA((64,)), pltpu.SemaphoreType.DMA((64,)),
                        pltpu.SemaphoreType.DMA((1,))],
        compiler_params=pltpu.CompilerParams(collective_id=1, has_side_effects=True, vmem_limit_bytes=58 << 20),
        name="ffn",
    )(nm, gu, dn, call, mid, rmid, mg)


def shards(tokens, documents, piece_starts, latent_down, key_value, query_up, output_weight, gate_weight, up_weight,
           down_weight, input_gain, latent_gain, middle_gain, cotangent):
    cos, sin = own_rope(256)
    lnst, lat, rlat, q, kv, w, mix, oall, mid, nm, rmid, gu, dn, call = attn_fwd(
        tokens, documents, piece_starts, latent_down, key_value, query_up, output_weight, input_gain[None],
        latent_gain[None], middle_gain[None], cos, sin, cotangent, jnp.pad(gate_weight, ((0, 0), (0, 128))),
        jnp.pad(up_weight, ((0, 0), (0, 128))), jnp.pad(down_weight, ((0, 128), (0, 0))))
    out, gmid, gain_mid, ggu, gdn = ffn(nm, gu, dn, call, mid, rmid, middle_gain[None])
    a = lax.psum_scatter(ggu.reshape(4, 8, 64, 768), "dp", scatter_dimension=1)
    b = lax.psum_scatter(gdn.reshape(4, 8, 48, 512), "dp", scatter_dimension=1)
    a = lax.all_to_all(a, "row", 0, 0, tiled=True)
    b = lax.all_to_all(b, "row", 0, 0, tiled=True)
    a = jnp.moveaxis(a, 0, 1)
    a = lax.all_gather(a, "dp", axis=0, tiled=True)
    b = lax.all_gather(b, "dp", axis=1)
    grad_gate = a[:, :, :384].reshape(512, 1536)[:, :1408].astype(F32)
    grad_up = a[:, :, 384:].reshape(512, 1536)[:, :1408].astype(F32)
    grad_down = b.reshape(1536, 512)[:1408].astype(F32)
    r, c = lax.axis_index("row"), lax.axis_index("col")
    gb = gmid.astype(BF)
    gb_all = lax.all_gather(gb, "row", axis=0)
    gmix = sum(jnp.dot(gb_all[k], oall[k].T, preferred_element_type=F32) for k in range(4)).astype(BF)
    gout = jnp.einsum("tm,ktn->mkn", mix, gb_all, preferred_element_type=F32).reshape(1024, 2048)
    gout = lax.psum_scatter(gout.astype(BF), "col", scatter_dimension=1, tiled=True)
    gout = lax.psum(gout, "dp").astype(F32)
    gmix = gmix.reshape(256, 4, 256)
    keys, values = kv[:, :256], kv[:, 256:]
    gw = jnp.einsum("qhd,kd->hqk", gmix, values, preferred_element_type=F32)
    wf = w.astype(F32)
    gs = (wf * (gw - jnp.sum(gw * wf, axis=2, keepdims=True))).astype(BF)
    gq = jnp.einsum("hqk,kd->qhd", gs, keys, preferred_element_type=F32) / 16.0
    gk = jnp.einsum("hqk,hqd->kd", gs, q, preferred_element_type=F32)
    gv = jnp.einsum("hqk,qhd->kd", w, gmix, preferred_element_type=F32)

    def un(g, cs, sn):
        a, b = g[..., :128], g[..., 128:]
        return jnp.concatenate([a * cs + b * sn, b * cs - a * sn], axis=-1)

    gqr = un(gq, cos[:, None], sin[:, None]).reshape(256, 1024).astype(BF)
    ln = lnst[:, :, :1024].reshape(256, 1024)
    r_in = jnp.sum(lnst[:, :, 1024:1027].astype(F32), axis=2).reshape(256, 1)
    gqu = jnp.dot(ln.T, gqr, preferred_element_type=F32)
    gln = lax.psum_scatter(jnp.dot(gqr, query_up.T, preferred_element_type=F32).astype(BF), "row",
                           scatter_dimension=0, tiled=True).astype(F32)
    gkv = lax.psum_scatter(jnp.concatenate([gk, gv], axis=1).astype(BF), ("col", "row"),
                           scatter_dimension=0, tiled=True).astype(F32)
    cs, sn = lax.dynamic_slice_in_dim(cos, r * 64, 64, 0), lax.dynamic_slice_in_dim(sin, r * 64, 64, 0)
    rl = rlat[:, :1]
    gained = gln * latent_gain
    glat = rl * gained - lat * (rl**3 * jnp.mean(gained * lat, axis=1, keepdims=True))
    glg = jnp.sum(gln * lat * rl, axis=0)
    glat = jnp.concatenate([glat, un(gkv[:, :256], cs, sn), gkv[:, 256:]], axis=1).astype(BF)
    glat = lax.all_gather(glat, "row", axis=0, tiled=True)
    x = tokens.astype(F32)
    normed = (x * r_in * input_gain).astype(BF)
    gld = jnp.dot(normed.T, glat, preferred_element_type=F32)
    gn = jnp.dot(glat[:, :1024], latent_down.T, preferred_element_type=F32)
    gn = gn + jnp.dot(glat[:, 1024:], key_value.T, preferred_element_type=F32)
    gained = gn * input_gain
    stat = lax.psum(jnp.sum(gained * x, axis=1, keepdims=True), "row")
    gx = gmid + r_in * gained - x * (r_in**3 * stat / D)
    gig = jnp.sum(gn * x * r_in, axis=0)
    gld, gqu = lax.psum((gld.astype(BF), gqu.astype(BF)), ("dp", "col"))
    gig, gmg = lax.psum((gig, gain_mid[0]), ("dp", "col"))
    glg = lax.psum(glg, ("dp", "row", "col"))
    return (out, gx.astype(BF), gld[:, :1024].astype(F32), gld[:, 1024:].astype(F32), gqu.astype(F32), gout,
            grad_gate, grad_up, grad_down, gig, glg, gmg)


def solution(mesh):
    placed = (P(("dp", "col"), "row"), P("dp", None), P("dp", None), P("row", None), P("row", None), P(None, "row"),
              P("row", "col"), P("row", "col"), P("row", "col"), P("col", "row"), P("row"), P(), P("row"),
              P(("dp", "col"), "row"))
    return jax.shard_map(
        shards, mesh=mesh, in_specs=placed,
        out_specs=(P(("dp", "col"), "row"), P(("dp", "col"), "row"), P("row", None), P("row", None), P(None, "row"),
                   P("row", "col"), P("row", "col"), P("row", "col"), P("col", "row"), P("row"), P(), P("row")),
        check_vma=False)
```

```python
import math

import jax
import jax.numpy as jnp
from jax import lax
from jax.experimental import pallas as pl
from jax.experimental.pallas import tpu as pltpu
from jax.sharding import PartitionSpec as P

D = 2048
SEQ = 1024
PIECE = 256
epsilon = 1e-06
masked_value = -1e30
F32 = jnp.float32
BF = jnp.bfloat16
MESH = pl.DeviceIdType.MESH
VM = pl.BlockSpec(memory_space=pltpu.VMEM)
SM = pl.BlockSpec(memory_space=pltpu.SMEM)
ANY = pl.BlockSpec(memory_space=pl.ANY)
NN = (((1,), (0,)), ((), ()))
NT = (((1,), (1,)), ((), ()))
TN = (((0,), (0,)), ((), ()))


def dot(a, b, dims=NN):
    return lax.dot_general(a, b, dims, preferred_element_type=F32)


class Links:
    def __init__(self, ssem, rsem, lsem):
        self.ssem, self.rsem, self.lsem = ssem, rsem, lsem
        self.n, self.m, self.open = 0, 0, []

    def send(self, src, dst, dev):
        c = pltpu.make_async_remote_copy(
            src_ref=src, dst_ref=dst, send_sem=self.ssem.at[self.n], recv_sem=self.rsem.at[self.n],
            device_id=dev, device_id_type=MESH)
        self.n += 1
        c.start()
        self.open.append(c)
        return c

    def local(self, src, dst):
        c = pltpu.make_async_copy(src, dst, self.lsem.at[self.m])
        self.m += 1
        c.start()
        return c

    def close(self):
        for c in self.open:
            c.wait_send()


def place():
    r, c = lax.axis_index("row"), lax.axis_index("col")
    core = {"col": c + 1 - 2 * lax.rem(c, 2)}
    yl = {"col": lax.rem(c + 2, 4)}
    zs = [{"row": lax.rem(r + k, 4)} for k in (1, 2, 3)]
    return r, c, core, yl, zs


def x_peers():
    p = lax.axis_index("dp")
    x = lax.rem(p, 4)
    return x, [{"dp": p - x + lax.rem(x + k, 4)} for k in (1, 2, 3)]


def blk(c):
    return pl.ds(pl.multiple_of(c * 256, 256), 256)


class Gather16:
    def __init__(self, net, buf):
        r, c, core, yl, zs = place()
        self.net, self.buf, self.at = net, buf, (r, c, core, yl, zs)

    def put(self, a, b, dev):
        v = self.buf.at[a, blk(b)]
        return self.net.send(v, v, dev)

    def first(self):
        r, c, core, yl, zs = self.at
        self.y = self.put(r, c, yl)
        self.z2 = self.put(r, c, zs[1])
        self.zp = self.put(r, c, zs[0])
        self.zm = self.put(r, c, zs[2])
        self.cores = [self.put(r, c, core)]

    def second(self):
        r, c, core, yl, zs = self.at
        far = lax.rem(c + 2, 4)
        self.y.wait_recv()
        self.yp = self.put(r, far, zs[0])
        self.ym = self.put(r, far, zs[2])
        self.cores.append(self.put(r, far, core))
        self.z2.wait_recv()
        self.zy = self.put(lax.rem(r + 2, 4), c, yl)
        self.cores.append(self.put(lax.rem(r + 2, 4), c, core))
        self.zp.wait_recv()
        self.cores.append(self.put(lax.rem(r + 3, 4), c, core))
        self.zm.wait_recv()
        self.cores.append(self.put(lax.rem(r + 1, 4), c, core))

    def third(self):
        r, c, core, yl, zs = self.at
        far = lax.rem(c + 2, 4)
        self.yp.wait_recv()
        self.cores.append(self.put(lax.rem(r + 3, 4), far, core))
        self.ym.wait_recv()
        self.cores.append(self.put(lax.rem(r + 1, 4), far, core))
        self.zy.wait_recv()
        self.cores.append(self.put(lax.rem(r + 2, 4), far, core))

    def last(self):
        for h in self.cores:
            h.wait_recv()


class Scatter16:
    def __init__(self, net, part, ctx, crx, tx, rx):
        self.net, self.part, self.at = net, part, place()
        self.ctx, self.crx, self.tx, self.rx = ctx, crx, tx, rx

    def first(self):
        r, c, core, yl, zs = self.at
        other = c + 1 - 2 * lax.rem(c, 2)
        self.cores = []
        for slot in (5, 7, 6, 1, 3, 2, 4, 0):
            b = other if slot < 4 else lax.rem(other + 2, 4)
            self.ctx[slot] = self.part(slot % 4, b).astype(BF)
            self.cores.append((slot, self.net.send(self.ctx.at[slot], self.crx.at[slot], core)))
        self.cores = dict(self.cores)

    def mine(self, slot):
        r, c, core, yl, zs = self.at
        b = c if slot < 4 else lax.rem(c + 2, 4)
        own = self.part(slot % 4, b)
        self.cores[slot].wait_recv()
        return own + self.crx[slot].astype(F32)

    def go(self, i, value, dev):
        self.tx[i] = value.astype(BF)
        return self.net.send(self.tx.at[i], self.rx.at[i], dev)

    def take(self, i, h):
        h.wait_recv()
        return self.rx[i].astype(F32)

    def second(self):
        r, c, core, yl, zs = self.at
        self.bp = self.go(0, self.mine(5), zs[0])
        self.bm = self.go(1, self.mine(7), zs[2])
        self.a = self.go(2, self.mine(6), yl)
        self.cp = self.go(3, self.mine(1), zs[0])
        self.cm = self.go(4, self.mine(3), zs[2])

    def third(self):
        r, c, core, yl, zs = self.at
        t = self.mine(2)
        self.d = self.go(5, t + self.take(2, self.a), zs[1])
        t = self.mine(4)
        self.e = self.go(6, t + self.take(0, self.bp) + self.take(1, self.bm), yl)

    def last(self):
        t = self.mine(0)
        for i, h in ((3, self.cp), (4, self.cm), (5, self.d), (6, self.e)):
            t = t + self.take(i, h)
        return t


class Weights:
    def __init__(self, net, gate, up, down, gu, dn):
        self.net, self.gate, self.up, self.down, self.gu, self.dn = net, gate, up, down, gu, dn
        self.x, self.xs = x_peers()

    def own(self):
        r = lax.axis_index("row")
        lanes = pl.ds(pl.multiple_of(r * 384, 128), 384)
        self.locals = [
            self.net.local(self.gate.at[:, lanes], self.gu.at[0, :, pl.ds(0, 384)]),
            self.net.local(self.up.at[:, lanes], self.gu.at[0, :, pl.ds(384, 384)]),
            self.net.local(self.down.at[pl.ds(pl.multiple_of(r * 384, 128), 384)], self.dn.at[0])]

    def first(self):
        r, c, core, yl, zs = place()
        x, net = self.x, self.net
        rows = pl.ds(pl.multiple_of(x * 128, 128), 128)
        self.z = []
        for k in (2, 1, 3):
            d = lax.rem(r + k, 4)
            lanes = pl.ds(pl.multiple_of(d * 384, 128), 384)
            drows = pl.ds(pl.multiple_of(d * 384 + x * 96, 32), 96)
            slot = 4 - k
            self.z += [
                net.send(self.gate.at[rows, lanes], self.gu.at[slot, rows, pl.ds(0, 384)], zs[k - 1]),
                net.send(self.up.at[rows, lanes], self.gu.at[slot, rows, pl.ds(384, 384)], zs[k - 1]),
                net.send(self.down.at[drows], self.dn.at[slot, pl.ds(pl.multiple_of(x * 96, 32), 96)], zs[k - 1])]

    def second(self):
        x, net = self.x, self.net
        for h in self.z:
            h.wait_recv()
        g = self.gu.at[pl.ds(1, 3), pl.ds(pl.multiple_of(x * 128, 128), 128)]
        d = self.dn.at[pl.ds(1, 3), pl.ds(pl.multiple_of(x * 96, 32), 96)]
        self.h = []
        for k in (2, 1, 3):
            self.h += [net.send(g, g, self.xs[k - 1]), net.send(d, d, self.xs[k - 1])]

    def last(self):
        for h in self.h:
            h.wait_recv()
        for h in self.locals:
            h.wait()


def meet(peers):
    b = pltpu.get_barrier_semaphore()
    for p in peers:
        pl.semaphore_signal(b, inc=1, device_id=p, device_id_type=MESH)
    pl.semaphore_wait(b, len(peers))


def pack_stat(s, lanes=128):
    hi = s.astype(BF).astype(F32)
    lo = (s - hi).astype(BF).astype(F32)
    rest = s - hi - lo
    lane = lax.broadcasted_iota(jnp.int32, (s.shape[0], lanes), 1)
    return jnp.where(lane == 0, hi, jnp.where(lane == 1, lo, jnp.where(lane == 2, rest, 0.0))).astype(BF)


def unpack_stat(t):
    return jnp.sum(t.astype(F32), axis=1, keepdims=True)


def rope(u, cos, sin):
    a, b = u[:, :128], u[:, 128:]
    return jnp.concatenate([a * cos - b * sin, b * cos + a * sin], axis=1)


def unrope(g, cos, sin):
    a, b = g[:, :128], g[:, 128:]
    return jnp.concatenate([a * cos + b * sin, b * cos - a * sin], axis=1)


def attn_fwd_kernel(x_ref, docs_ref, starts_ref, ld_ref, kvw_ref, qu_hbm, ow_hbm, ig_ref, lg_ref, mg_ref,
                    cos_ref, sin_ref, cot_ref, gate_hbm, up_hbm, down_hbm,
                    ln_ref, lat_ref, rlat_ref, q_ref, kv_ref, w_ref, mix_ref, oall_ref, mid_ref, nm_ref, rmid_ref,
                    gu_ref, dn_ref, call_ref,
                    pf, ps, prx, qu_v, bias, bp, brx, st_tx, st_rx, ssem, rsem, lsem):
    r, c, core, yl, zs = place()
    net = Links(ssem, rsem, lsem)
    meet(zs + [core, yl] + x_peers()[1])
    ow_own = net.local(ow_hbm, oall_ref.at[c])
    ow_yl = net.send(ow_hbm, oall_ref.at[c], yl)
    ow_core = net.send(ow_hbm, oall_ref.at[c], core)
    qu_in = net.local(qu_hbm, qu_v)
    ffw = Weights(net, gate_hbm, up_hbm, down_hbm, gu_ref, dn_ref)
    ffw.own()
    call_ref[r, blk(c)] = cot_ref[...]
    cots = Gather16(net, call_ref)

    x = x_ref[...].astype(F32)
    xg = (x * ig_ref[...]).astype(BF)
    ssq = jnp.sum(x * x, axis=1, keepdims=True)
    pf[:, :1024] = dot(xg, ld_ref[...])
    pf[:, 1024:1536] = dot(xg, kvw_ref[...])
    pf[:, 1536:] = jnp.broadcast_to(ssq, (256, 128))
    stat = pack_stat(ssq)
    for d in range(4):
        rows = slice(64 * d, 64 * d + 64)
        ps[d, :, :1536] = pf[rows, :1536].astype(BF)
        ps[d, :, 1536:] = stat[rows]
    got = []
    for k in (2, 1, 3):
        got.append(net.send(ps.at[lax.rem(r + k, 4)], prx.at[k - 1], zs[k - 1]))

    qpos = c * 256 + lax.broadcasted_iota(jnp.int32, (256, SEQ), 0)
    kpos = lax.broadcasted_iota(jnp.int32, (256, SEQ), 1)
    number = lax.broadcasted_iota(jnp.int32, (8, SEQ), 0)
    onehot = (jnp.broadcast_to(docs_ref[...], (8, SEQ)) == number).astype(F32)
    onehot_q = (jnp.broadcast_to(docs_ref[:, pl.ds(pl.multiple_of(c * 256, 256), 256)], (8, 256))
                == number[:, :256]).astype(F32)
    same_doc = dot(onehot_q, onehot, TN) > 0.5
    ok = kpos <= qpos
    for m in range(2):
        s = starts_ref[0, m]
        ok = ok | ((qpos >= s) & (qpos < s + PIECE) & (kpos >= s) & (kpos < s + PIECE))
    bias[...] = jnp.where(same_doc & ok, 0.0, masked_value)

    own = pl.ds(pl.multiple_of(r * 64, 64), 64)
    for g in got:
        g.wait_recv()
    total = pf[own, :1536]
    ss = pf[own, 1536:1537]
    for k in range(3):
        total = total + prx[k, :, :1536].astype(F32)
        ss = ss + unpack_stat(prx[k, :, 1536:])
    r_in = lax.rsqrt(ss / D + epsilon)
    total = total * r_in
    cos64, sin64 = cos_ref[own, :], sin_ref[own, :]
    kv_rows = pl.ds(pl.multiple_of(c * 256 + r * 64, 64), 64)
    kv_ref[kv_rows, :256] = rope(total[:, 1024:1280], cos64, sin64).astype(BF)
    kv_ref[kv_rows, 256:] = total[:, 1280:1536].astype(BF)
    kv_got = [net.send(kv_ref.at[kv_rows], kv_ref.at[kv_rows], zs[k - 1]) for k in (2, 1, 3)]
    lat = total[:, :1024]
    r_lat = lax.rsqrt(jnp.mean(lat * lat, axis=1, keepdims=True) + epsilon)
    ln_ref[r, :, :1024] = (lat * r_lat * lg_ref[...]).astype(BF)
    ln_ref[r, :, 1024:] = pack_stat(r_in)
    ln_got = [net.send(ln_ref.at[r], ln_ref.at[r], zs[k - 1]) for k in (2, 1, 3)]
    lat_ref[...] = lat
    rlat_ref[...] = jnp.broadcast_to(r_lat, (64, 128))
    for g in kv_got:
        g.wait_recv()
    own_kv = kv_ref.at[pl.ds(pl.multiple_of(c * 256, 256), 256)]
    kv_yl = net.send(own_kv, own_kv, yl)
    kv_core = net.send(own_kv, own_kv, core)
    for g in ln_got:
        g.wait_recv()
    ffw.first()
    cots.first()
    qu_in.wait()
    cos, sin = cos_ref[...], sin_ref[...]
    ln_all = ln_ref[:, :, :1024].reshape(256, 1024)

    def make_query(h, carry):
        u = dot(ln_all, qu_v[:, pl.ds(pl.multiple_of(h * 256, 256), 256)])
        q_ref[h] = (rope(u, cos, sin) * (1.0 / 16.0)).astype(BF)
        return carry

    lax.fori_loop(0, 4, make_query, 0)
    kv_yl.wait_recv()
    far_kv = kv_ref.at[pl.ds(pl.multiple_of(lax.rem(c + 2, 4) * 256, 256), 256)]
    kv_far = net.send(far_kv, far_kv, core)
    ow_yl.wait_recv()
    ow_far = net.send(oall_ref.at[lax.rem(c + 2, 4)], oall_ref.at[lax.rem(c + 2, 4)], core)
    kv_core.wait_recv()
    kv_far.wait_recv()

    def head(h, carry):
        s = dot(q_ref[h], kv_ref[:, :256], NT) + bias[...]
        top = jnp.max(s, axis=1, keepdims=True)
        e = jnp.exp(s - top)
        w = (e / jnp.sum(e, axis=1, keepdims=True)).astype(BF)
        w_ref[h] = w
        mix_ref[:, pl.ds(pl.multiple_of(h * 256, 256), 256)] = dot(w, kv_ref[:, 256:]).astype(BF)
        return carry

    lax.fori_loop(0, 4, head, 0)
    ffw.second()
    cots.second()
    ow_own.wait()
    ow_core.wait_recv()
    ow_far.wait_recv()
    got = []
    for k in (2, 1, 3):
        d = lax.rem(r + k, 4)
        bp[k - 1] = dot(mix_ref[...], oall_ref[d]).astype(BF)
        got.append(net.send(bp.at[k - 1], brx.at[k - 1], zs[k - 1]))
    branch = dot(mix_ref[...], oall_ref[r])
    for g in got:
        g.wait_recv()
    for k in range(3):
        branch = branch + brx[k].astype(F32)
    middle = x_ref[...].astype(F32) + branch
    mid_ref[...] = middle
    ssm = jnp.sum(middle * middle, axis=1, keepdims=True)
    st_tx[...] = jnp.broadcast_to(ssm, (256, 128))
    got = [net.send(st_tx, st_rx.at[k - 1], zs[k - 1]) for k in (2, 1, 3)]
    for g in got:
        g.wait_recv()
    for k in range(3):
        ssm = ssm + st_rx[k, :, :1]
    r_mid = lax.rsqrt(ssm / D + epsilon)
    rmid_ref[...] = jnp.broadcast_to(r_mid, (256, 128))
    nm_ref[...] = (middle * r_mid * mg_ref[...]).astype(BF)
    cots.third()
    cots.last()
    ffw.last()
    net.close()


def S(shape, dtype=BF):
    return jax.ShapeDtypeStruct(shape, dtype)


def attn_fwd(x, docs, starts, ld, kvw, qu, ow, ig, lg, mg, cos, sin, cot, gate, up, down):
    return pl.pallas_call(
        attn_fwd_kernel,
        out_shape=(S((4, 64, 1152)), S((64, 1024), F32), S((64, 128), F32), S((4, 256, 256)), S((1024, 512)),
                   S((4, 256, 1024)), S((256, 1024)), S((4, 1024, 512)), S((256, 512), F32), S((256, 512)),
                   S((256, 128), F32), S((4, 512, 768)), S((4, 384, 512)), S((4, 1024, 512))),
        in_specs=[VM, VM, SM, VM, VM, ANY, ANY, VM, VM, VM, VM, VM, VM, ANY, ANY, ANY],
        out_specs=(VM,) * 14,
        scratch_shapes=[
            pltpu.VMEM((256, 1664), F32), pltpu.VMEM((4, 64, 1664), BF), pltpu.VMEM((3, 64, 1664), BF),
            pltpu.VMEM((1024, 1024), BF), pltpu.VMEM((256, 1024), F32), pltpu.VMEM((3, 256, 512), BF),
            pltpu.VMEM((3, 256, 512), BF), pltpu.VMEM((256, 128), F32), pltpu.VMEM((3, 256, 128), F32),
            pltpu.SemaphoreType.DMA((64,)), pltpu.SemaphoreType.DMA((64,)), pltpu.SemaphoreType.DMA((8,))],
        compiler_params=pltpu.CompilerParams(collective_id=0, has_side_effects=True, vmem_limit_bytes=56 << 20),
        name="attn_fwd",
    )(x, docs, starts, ld, kvw, qu, ow, ig, lg, mg, cos, sin, cot, gate, up, down)


def own_rope(local_rows):
    places = lax.axis_index("col") * local_rows + jnp.arange(local_rows, dtype=jnp.int32)
    freq = jnp.exp(-math.log(10000.0) * jnp.arange(128, dtype=F32) / 128)
    ang = places.astype(F32)[:, None] * freq[None, :]
    return jnp.cos(ang), jnp.sin(ang)


def ffn_kernel(nm_ref, gu_ref, dn_ref, call_ref, mid_ref, rmid_ref, mg_ref,
               out_ref, gmid_ref, gain_ref, ggu_out, gdn_out,
               m_ref, act_ref, gg_ref, ctx1, crx1, tx1, rx1, ctx2, crx2, tx2, rx2, st_tx, st_rx, ssem, rsem, lsem):
    r, c, core, yl, zs = place()
    net = Links(ssem, rsem, lsem)
    m_ref[r, blk(c)] = nm_ref[...]
    meet(zs + [core, yl])
    gather = Gather16(net, m_ref)
    gather.first()
    gather.second()
    gather.third()
    gather.last()

    def tile(t, carry):
        rows = blk(t)
        gu = jnp.zeros((256, 768), F32)
        ga = jnp.zeros((256, 384), F32)
        for k in range(4):
            f = lax.rem(r + k, 4)
            gu = gu + dot(m_ref[f, rows], gu_ref[k])
            ga = ga + dot(call_ref[f, rows], dn_ref[k], NT)
        g, u = gu[:, :384], gu[:, 384:]
        sig = 1.0 / (1.0 + jnp.exp(-g))
        silu = g * sig
        act_ref[rows] = (silu * u).astype(BF)
        gg_ref[rows, :384] = (ga * u * sig * (1.0 + g * (1.0 - sig))).astype(BF)
        gg_ref[rows, 384:] = (ga * silu).astype(BF)
        return carry

    lax.fori_loop(0, 4, tile, 0)
    back = Scatter16(net, lambda k, b: dot(gg_ref[blk(b)], gu_ref[k], NT), ctx1, crx1, tx1, rx1)
    back.first()
    back.second()

    def grads(k, carry):
        f = lax.rem(r + k, 4)
        ggu_out[f] = dot(m_ref[f], gg_ref[...], TN).astype(BF)
        gdn_out[f] = dot(act_ref[...], call_ref[f], TN).astype(BF)
        return carry

    lax.fori_loop(0, 2, grads, 0)
    back.third()
    lax.fori_loop(2, 4, grads, 0)
    fwd = Scatter16(net, lambda k, b: dot(act_ref[blk(b)], dn_ref[k]), ctx2, crx2, tx2, rx2)
    fwd.first()
    gm = back.last()
    middle, r_mid = mid_ref[...], rmid_ref[:, :1]
    gained = gm * mg_ref[...]
    stat = jnp.sum(gained * middle, axis=1, keepdims=True)
    st_tx[...] = jnp.broadcast_to(stat, (256, 128))
    got = [net.send(st_tx, st_rx.at[k - 1], zs[k - 1]) for k in (2, 1, 3)]
    gain_ref[...] = jnp.sum(gm * middle * r_mid, axis=0, keepdims=True)
    fwd.second()
    for g in got:
        g.wait_recv()
    for k in range(3):
        stat = stat + st_rx[k, :, :1]
    gmid_ref[...] = call_ref[r, blk(c)].astype(F32) + r_mid * gained - middle * (r_mid * r_mid * r_mid * stat / D)
    fwd.third()
    out_ref[...] = (middle + fwd.last()).astype(BF)
    net.close()


def ffn(nm, gu, dn, call, mid, rmid, mg):
    big = [pltpu.VMEM((8, 256, 512), BF), pltpu.VMEM((8, 256, 512), BF), pltpu.VMEM((7, 256, 512), BF),
           pltpu.VMEM((7, 256, 512), BF)]
    return pl.pallas_call(
        ffn_kernel,
        out_shape=(S((256, 512)), S((256, 512), F32), S((1, 512), F32), S((4, 512, 768)), S((4, 384, 512))),
        in_specs=[VM] * 7,
        out_specs=(VM,) * 5,
        scratch_shapes=[pltpu.VMEM((4, 1024, 512), BF), pltpu.VMEM((1024, 384), BF), pltpu.VMEM((1024, 768), BF),
                        *big, *big, pltpu.VMEM((256, 128), F32), pltpu.VMEM((3, 256, 128), F32),
                        pltpu.SemaphoreType.DMA((64,)), pltpu.SemaphoreType.DMA((64,)),
                        pltpu.SemaphoreType.DMA((1,))],
        compiler_params=pltpu.CompilerParams(collective_id=1, has_side_effects=True, vmem_limit_bytes=58 << 20),
        name="ffn",
    )(nm, gu, dn, call, mid, rmid, mg)


def rows_of(start, n):
    return pl.ds(pl.multiple_of(start, n & -n), n)


def ring_scatter(net, src, tx, rx, x, xs):
    f = lambda v: v[...].astype(F32)
    n1, n2, n3 = (lax.rem(x + k, 4) for k in (1, 2, 3))
    m1 = net.send(src(n2, 0), rx.at[0], xs[0])
    m2 = net.send(src(n2, 1), rx.at[1], xs[2])
    m3 = net.send(src(n1, 1), rx.at[2], xs[0])
    m4 = net.send(src(n3, 0), rx.at[3], xs[2])
    yield
    m1.wait_recv()
    tx[0] = (f(src(n1, 0)) + f(rx.at[0])).astype(BF)
    m5 = net.send(tx.at[0], rx.at[4], xs[0])
    m2.wait_recv()
    tx[1] = (f(src(n3, 1)) + f(rx.at[1])).astype(BF)
    m6 = net.send(tx.at[1], rx.at[5], xs[2])
    yield
    m3.wait_recv()
    m4.wait_recv()
    m5.wait_recv()
    m6.wait_recv()
    return f(src(x, 0)) + f(rx.at[3]) + f(rx.at[4]), f(src(x, 1)) + f(rx.at[2]) + f(rx.at[5])


def ring_gather(net, view, x, xs):
    n1, n3 = lax.rem(x + 1, 4), lax.rem(x + 3, 4)
    p = net.send(view(x, None), view(x, None), xs[0])
    m = net.send(view(x, None), view(x, None), xs[2])
    yield
    p.wait_recv()
    p = net.send(view(n3, 0), view(n3, 0), xs[0])
    m.wait_recv()
    m = net.send(view(n1, 1), view(n1, 1), xs[2])
    yield
    p.wait_recv()
    m.wait_recv()


def pair_scatter(net, both, rx, bit, dev):
    h = net.send(both.at[1 - bit], rx, dev)
    yield
    h.wait_recv()
    return both[bit].astype(F32) + rx[...].astype(F32)


def pair_gather(net, view, dev):
    h = net.send(view, view, dev)
    yield
    h.wait_recv()


def reduce_dp(net, at, src, buf, fin, n, spread):
    x, xs, yh, yhd = at
    tx, rx, both, prx = buf
    a, b = yield from ring_scatter(net, src, tx, rx, x, xs)
    both[0] = a.astype(BF)
    both[1] = b.astype(BF)
    t = yield from pair_scatter(net, both, prx, yh, yhd)
    piece = rows_of(x * 2 * n + yh * n, n)
    yield from spread(t, piece)
    yield from pair_gather(net, fin(piece), yhd)

    def view(j, h):
        return fin(rows_of(j * 2 * n, 2 * n) if h is None else rows_of(j * 2 * n + h * n, n))

    yield from ring_gather(net, view, x, xs)


def reduce_all(net, at, part, buf, fin):
    x, xs, yh, yhd, core, coredev, yl, yldev = at
    crx, csum, tx, rx, both, yrx, both2, prx = buf
    half = part.shape[0] // 2
    n = half // 8
    h = net.send(part.at[rows_of((1 - core) * half, half)], crx, coredev)
    yield
    h.wait_recv()
    csum[...] = (part[rows_of(core * half, half)].astype(F32) + crx[...].astype(F32)).astype(BF)
    a, b = yield from ring_scatter(net, lambda j, h: csum.at[rows_of(j * 2 * n + h * n, n)], tx, rx, x, xs)
    both[0] = a.astype(BF)
    both[1] = b.astype(BF)
    t = yield from pair_scatter(net, both, yrx, yl, yldev)
    both2[0] = t[:n // 2].astype(BF)
    both2[1] = t[n // 2:].astype(BF)
    t = yield from pair_scatter(net, both2, prx, yh, yhd)
    base = core * half + x * 2 * n + yl * n
    fin[rows_of(base + yh * (n // 2), n // 2)] = t.astype(BF)
    v = fin.at[rows_of(base + yh * (n // 2), n // 2)]
    yield from pair_gather(net, v, yhd)
    yield from pair_gather(net, fin.at[rows_of(base, n)], yldev)

    def view(j, h):
        s = core * half + j * 2 * n
        return fin.at[rows_of(s, 2 * n)] if h is None else fin.at[rows_of(s + h * n, n)]

    yield from ring_gather(net, view, x, xs)
    yield from pair_gather(net, fin.at[rows_of(core * half, half)], coredev)


def reduce_vec(net, at, zs, v, rx):
    x, xs, yh, yhd, core, coredev, yl, yldev = at
    hs = [net.send(v.at[0], rx.at[k], zs[k]) for k in range(3)]
    yield
    for h in hs:
        h.wait_recv()
    low = lax.broadcasted_iota(jnp.int32, (8, 256), 0) < 4
    v[1] = v[0] + jnp.where(low, 0.0, rx[0] + rx[1] + rx[2])
    for i, dev in ((1, coredev), (2, yldev), (3, yhd)):
        h = net.send(v.at[i], rx.at[2 + i], dev)
        yield
        h.wait_recv()
        v[i + 1] = v[i] + rx[2 + i]
    hs = [net.send(v.at[4], rx.at[6 + k], xs[k]) for k in range(3)]
    yield
    for h in hs:
        h.wait_recv()
    v[5] = v[4] + rx[6] + rx[7] + rx[8]


def step(*gens):
    for g in gens:
        next(g, None)


def finish(*gens):
    live = list(gens)
    done = object()
    while live:
        live = [g for g in live if next(g, done) is not done]


def attn_bwd_kernel(gmid_ref, oall_hbm, w_ref, q_ref, kv_ref, mix_ref, ln_ref, lat_ref, rlat_ref, qu_hbm, ld_ref,
                    kvw_ref, x_ref, cos_ref, sin_ref, ig_ref, lg_ref, gmg_ref, ggu_ref, gdn_ref,
                    gx_ref, fgu_ref, fdn_ref, fout_ref, fqu_ref, fld_ref, vec_ref,
                    oall_ref, qu_v, gb, gmx, gqr, acc, kvt, kvrx, glt, glrx, glat, st_tx, st_rx,
                    gocrx, goyrx, pqu, pld, vec, vrx,
                    utx, urx, ub, uprx, upc, dtx, drx, db, dprx, dpc, otx, orx, ob, oprx,
                    qcrx, qcs, qtx, qrx, qb, qyrx, qb2, qprx, lcrx, lcs, ltx, lrx, lb, lyrx, lb2, lprx,
                    ssem, rsem, lsem):
    r, c, coredev, yldev, zs = place()
    x, xs = x_peers()
    p = lax.axis_index("dp")
    yh, yhd = p // 4, {"dp": lax.rem(p + 4, 8)}
    core, yl = lax.rem(c, 2), c // 2
    at, at_all = (x, xs, yh, yhd), (x, xs, yh, yhd, core, coredev, yl, yldev)
    others = [(j % 4, j // 4) for j in range(1, 16)]
    group = [{"row": lax.rem(r + i, 4), "col": lax.rem(c + j, 4)} for i, j in others]
    net = Links(ssem, rsem, lsem)
    oall_in = net.local(oall_hbm, oall_ref)
    qu_in = net.local(qu_hbm, qu_v)
    gop, goytx, gosum = oall_ref.at[pl.ds(0, 2)], oall_ref.at[2], oall_ref.at[3]
    gb[r] = gmid_ref[...].astype(BF)
    meet(group + xs + [yhd])
    got = [net.send(gb.at[r], gb.at[r], zs[k - 1]) for k in (2, 1, 3)]

    def spread_to(pc, fin):
        def spread(t, piece):
            pc[...] = t.astype(BF)
            hs = [net.send(pc.at[lax.rem(r + k, 4)], fin.at[r, piece], zs[k - 1]) for k in (2, 1, 3)]
            fin[r, piece] = pc[r]
            yield
            for h in hs:
                h.wait_recv()
        return spread

    red_u = reduce_dp(net, at, lambda j, h: ggu_ref.at[:, rows_of(j * 128 + h * 64, 64)], (utx, urx, ub, uprx),
                      lambda rows: fgu_ref.at[:, rows], 64, spread_to(upc, fgu_ref))
    red_d = reduce_dp(net, at, lambda j, h: gdn_ref.at[:, rows_of(j * 96 + h * 48, 48)], (dtx, drx, db, dprx),
                      lambda rows: fdn_ref.at[:, rows], 48, spread_to(dpc, fdn_ref))
    step(red_d, red_u)
    oall_in.wait()
    for g in got:
        g.wait_recv()

    def mixed_grad(h, carry):
        t = jnp.zeros((256, 256), F32)
        for k in range(4):
            t = t + dot(gb[k], oall_ref[k, blk(h)], NT)
        gmx[h] = t.astype(BF)
        return carry

    lax.fori_loop(0, 4, mixed_grad, 0)

    def out_block(b, t):
        return dot(mix_ref[:, blk(t)], gb[b], TN)

    def to_core(t, carry):
        for i in range(2):
            b = lax.rem(c + 1 - 2 * core + 2 * i, 4)
            gop[i, blk(t)] = out_block(b, t).astype(BF)
        return carry

    def from_core(t, carry):
        goytx[blk(t)] = (out_block(lax.rem(c + 2, 4), t) + gocrx[1, blk(t)].astype(F32)).astype(BF)
        gosum[blk(t)] = (out_block(c, t) + gocrx[0, blk(t)].astype(F32)).astype(BF)
        return carry

    def from_y(t, carry):
        gosum[blk(t)] = (gosum[blk(t)].astype(F32) + goyrx[blk(t)].astype(F32)).astype(BF)
        return carry

    def reduce_out():
        lax.fori_loop(0, 4, to_core, 0)
        h = net.send(gop, gocrx, coredev)
        yield
        h.wait_recv()
        lax.fori_loop(0, 4, from_core, 0)
        h = net.send(goytx, goyrx, yldev)
        yield
        h.wait_recv()
        lax.fori_loop(0, 4, from_y, 0)

        def spread(t, piece):
            fout_ref[piece] = t.astype(BF)
            return
            yield

        yield from reduce_dp(net, at, lambda j, h: gosum.at[rows_of(j * 256 + h * 128, 128)], (otx, orx, ob, oprx),
                             lambda rows: fout_ref.at[rows], 128, spread)

    red_o = reduce_out()
    step(red_o)

    acc[...] = jnp.zeros_like(acc)

    def head(h, carry):
        gm = gmx[h]
        gw = dot(gm, kv_ref[:, 256:], NT)
        w = w_ref[h]
        wf = w.astype(F32)
        t = wf * gw
        gs = (t - wf * jnp.sum(t, axis=1, keepdims=True)).astype(BF)
        gq = dot(gs, kv_ref[:, :256]) * (1.0 / 16.0)
        gqr[:, blk(h)] = unrope(gq, cos_ref[...], sin_ref[...]).astype(BF)
        acc[:, :256] += dot(gs, q_ref[h], TN)
        acc[:, 256:] += dot(w, gm, TN)
        return carry

    lax.fori_loop(0, 4, head, 0)
    kvt[...] = acc[...].astype(BF)
    kv_got = []
    for i, (a, b) in enumerate(others):
        rows = rows_of(lax.rem(c + b, 4) * 256 + lax.rem(r + a, 4) * 64, 64)
        kv_got.append(net.send(kvt.at[rows], kvrx.at[i], group[i]))
    qu_in.wait()

    def latent_grad(t, carry):
        glt[:, blk(t)] = dot(gqr[...], qu_v[blk(t)], NT).astype(BF)
        return carry

    lax.fori_loop(0, 4, latent_grad, 0)
    gl_got = [net.send(glt.at[rows_of(lax.rem(r + k, 4) * 64, 64)], glrx.at[k - 1], zs[k - 1]) for k in (2, 1, 3)]
    step(red_o)

    def query_up_grad(t, carry):
        pqu[blk(t)] = dot(ln_ref[:, :, blk(t)].reshape(256, 256), gqr[...], TN).astype(BF)
        return carry

    lax.fori_loop(0, 4, query_up_grad, 0)
    red_q = reduce_all(net, at_all, pqu, (qcrx, qcs, qtx, qrx, qb, qyrx, qb2, qprx), fqu_ref)
    step(red_q)

    own = rows_of(r * 64, 64)
    mine = acc[rows_of(c * 256 + r * 64, 64)]
    for i, h in enumerate(kv_got):
        h.wait_recv()
        mine = mine + kvrx[i].astype(F32)
    gl = glt[own].astype(F32)
    for i, h in enumerate(gl_got):
        h.wait_recv()
    for k in range(3):
        gl = gl + glrx[k].astype(F32)
    lat, rl = lat_ref[...], rlat_ref[:, :1]
    gained = gl * lg_ref[...]
    glat[r, :, :1024] = (rl * gained - lat * (rl * rl * rl * jnp.mean(gained * lat, axis=1, keepdims=True))).astype(BF)
    glat[r, :, 1024:1280] = unrope(mine[:, :256], cos_ref[own], sin_ref[own]).astype(BF)
    glat[r, :, 1280:] = mine[:, 256:].astype(BF)
    la_got = [net.send(glat.at[r], glat.at[r], zs[k - 1]) for k in (2, 1, 3)]
    glg = jnp.sum(gl * lat * rl, axis=0, keepdims=True)
    step(red_d, red_u, red_q)
    for h in la_got:
        h.wait_recv()
    g_all = glat[...].reshape(256, 1536)
    xf = x_ref[...].astype(F32)
    r_in = unpack_stat(ln_ref[:, :, 1024:].reshape(256, 128))
    gn = dot(g_all[:, :1024], ld_ref[...], NT) + dot(g_all[:, 1024:], kvw_ref[...], NT)
    gained = gn * ig_ref[...]
    stat = jnp.sum(gained * xf, axis=1, keepdims=True)
    st_tx[...] = jnp.broadcast_to(stat, (256, 128))
    st_got = [net.send(st_tx, st_rx.at[k - 1], zs[k - 1]) for k in (2, 1, 3)]
    normed = (xf * r_in * ig_ref[...]).astype(BF)
    pld[...] = dot(normed, g_all, TN).astype(BF)
    red_l = reduce_all(net, at_all, pld, (lcrx, lcs, ltx, lrx, lb, lyrx, lb2, lprx), fld_ref)
    step(red_l)
    gig = jnp.sum(gn * xf * r_in, axis=0, keepdims=True)
    for i in range(2):
        vec[0, i:i + 1] = gig[:, 256 * i:256 * i + 256]
        vec[0, 2 + i:3 + i] = gmg_ref[:, 256 * i:256 * i + 256]
    for i in range(4):
        vec[0, 4 + i:5 + i] = glg[:, 256 * i:256 * i + 256]
    red_v = reduce_vec(net, at_all, zs, vec, vrx)
    step(red_v)
    for h in st_got:
        h.wait_recv()
    for k in range(3):
        stat = stat + st_rx[k, :, :1]
    gx_ref[...] = (gmid_ref[...] + r_in * gained - xf * (r_in * r_in * r_in * stat / D)).astype(BF)
    finish(red_l, red_v, red_q, red_o, red_d, red_u)
    vec_ref[...] = vec[5]
    net.close()


def attn_bwd(*args):
    def ring(*shape):
        return [pltpu.VMEM((2, *shape), BF), pltpu.VMEM((6, *shape), BF), pltpu.VMEM((2, *shape), BF),
                pltpu.VMEM(shape, BF)]

    def whole(half, lanes):
        n = half // 8
        return [pltpu.VMEM((half, lanes), BF), pltpu.VMEM((half, lanes), BF), *ring(n, lanes),
                pltpu.VMEM((2, n // 2, lanes), BF), pltpu.VMEM((n // 2, lanes), BF)]

    v = pltpu.VMEM
    return pl.pallas_call(
        attn_bwd_kernel,
        out_shape=(S((256, 512)), S((4, 512, 768)), S((4, 384, 512)), S((1024, 512)), S((1024, 1024)),
                   S((512, 1536)), S((8, 256), F32)),
        in_specs=[VM, ANY] + [VM] * 7 + [ANY] + [VM] * 10,
        out_specs=(VM,) * 7,
        scratch_shapes=[
            v((4, 1024, 512), BF), v((1024, 1024), BF), v((4, 256, 512), BF), v((4, 256, 256), BF), v((256, 1024), BF), v((1024, 512), F32),
            v((1024, 512), BF), v((15, 64, 512), BF), v((256, 1024), BF), v((3, 64, 1024), BF), v((4, 64, 1536), BF),
            v((256, 128), F32), v((3, 256, 128), F32),
            v((2, 1024, 512), BF), v((1024, 512), BF),
            v((1024, 1024), BF), v((512, 1536), BF), v((6, 8, 256), F32), v((9, 8, 256), F32),
            *ring(4, 64, 768), v((4, 64, 768), BF), *ring(4, 48, 512), v((4, 48, 512), BF), *ring(128, 512),
            *whole(512, 1024), *whole(256, 1536),
            pltpu.SemaphoreType.DMA((144,)), pltpu.SemaphoreType.DMA((144,)), pltpu.SemaphoreType.DMA((2,))],
        compiler_params=pltpu.CompilerParams(collective_id=2, has_side_effects=True, vmem_limit_bytes=62 << 20),
        name="attn_bwd",
    )(*args)


def shards(tokens, documents, piece_starts, latent_down, key_value, query_up, output_weight, gate_weight, up_weight,
           down_weight, input_gain, latent_gain, middle_gain, cotangent):
    cos, sin = own_rope(256)
    ig, lg, mg = input_gain[None], latent_gain[None], middle_gain[None]
    lnst, lat, rlat, q, kv, w, mix, oall, mid, nm, rmid, gu, dn, call = attn_fwd(
        tokens, documents, piece_starts, latent_down, key_value, query_up, output_weight, ig, lg, mg, cos, sin,
        cotangent, jnp.pad(gate_weight, ((0, 0), (0, 128))),
        jnp.pad(up_weight, ((0, 0), (0, 128))), jnp.pad(down_weight, ((0, 128), (0, 0))))
    out, gmid, gain_mid, ggu, gdn = ffn(nm, gu, dn, call, mid, rmid, mg)
    gx, fgu, fdn, fout, fqu, fld, vec = attn_bwd(
        gmid, oall, w, q, kv, mix, lnst, lat, rlat, query_up, latent_down, key_value, tokens, cos, sin, ig, lg,
        gain_mid, ggu, gdn)
    wide = jnp.moveaxis(fgu, 0, 1)
    return (out, gx, fld[:, :1024].astype(F32), fld[:, 1024:].astype(F32), fqu.astype(F32), fout.astype(F32),
            wide[:, :, :384].reshape(512, 1536)[:, :1408].astype(F32),
            wide[:, :, 384:].reshape(512, 1536)[:, :1408].astype(F32),
            fdn.reshape(1536, 512)[:1408].astype(F32),
            vec[0:2].reshape(512), vec[4:8].reshape(1024), vec[2:4].reshape(512))


def solution(mesh):
    placed = (P(("dp", "col"), "row"), P("dp", None), P("dp", None), P("row", None), P("row", None), P(None, "row"),
              P("row", "col"), P("row", "col"), P("row", "col"), P("col", "row"), P("row"), P(), P("row"),
              P(("dp", "col"), "row"))
    return jax.shard_map(
        shards, mesh=mesh, in_specs=placed,
        out_specs=(P(("dp", "col"), "row"), P(("dp", "col"), "row"), P("row", None), P("row", None), P(None, "row"),
                   P("row", "col"), P("row", "col"), P("row", "col"), P("col", "row"), P("row"), P(), P("row")),
        check_vma=False)
```
